32 devices in a mesh: copy: 2 (over x), tm: 2 (over core), space: 8 (over z, y).
Axes of the slice: x: 2, y: 2, z: 4, core: 2. Of those that a mesh axis runs over, the one named last changes fastest.
Arguments:
- initial: float32 [4, 16, 128, 128], P(('copy', 'tm'), 'space'), parts along dimension 0, may hold values from 0.1 to 2
- source: bfloat16 [4, 16, 128, 128], P(('copy', 'tm'), 'space'), parts along dimension 0, may hold values from 0.049804688 to 1
- diffusion: float32 [16, 128, 128], P('space'), may hold values from 0.02 to 0.5
- wind_field: float32 [3, 16, 128, 128], P(None, 'space'), may hold values from -0.6 to 0.6
- buildings: int32 [16, 128, 128], P('space'), may hold values from 0 to 1, as said below
- strength: float32 [2, 4], P('tm'), may hold values from 0.5 to 2
Outputs:
- advanced: float32 [4, 16, 128, 128], P(('copy', 'tm'), 'space'), parts along dimension 0
- final_fine: float32 [4, 16, 128, 128], P(('copy', 'tm'), 'space'), parts along dimension 0
The draws below stay inside these ranges and needn't reach their ends.
There are 2 independent parts, one for each index of `copy`. The reference program is written for one: setup_inputs(seed, part) draws one part's arguments, and reference() takes and returns one part's arrays. A program takes and returns all parts, laid end to end along the dimension named above; an argument that names none is the same for every part. Nothing has to cross between parts.
Inputs may be any that keep to these rules, and one draw needn't show every extreme that they name: buildings stand on the ground as columns.
All inputs are finite; a program needn't handle non-finite values.
Results may differ from the reference program's by a relative error of at most 0.0003.
Values sent between devices are 32-bit elements; how exact they have to be, the bound alone decides.
A program may use at most 64 MiB of HBM per device.

```python
import math
import jax
import jax.numpy as jnp
from jax import lax

NY = 128
NZ = 128
FINE = 4
NX = 16
BLOCKS = 2


def draw_diffusion(key, part):
    first_key, second_key = jax.random.split(key, 2)
    center = jax.random.uniform(first_key, (), minval=0.0, maxval=1.0)
    places = (jnp.arange(NX, dtype=jnp.float32) + 0.5) / NX
    spread = 0.2
    logs = jax.random.uniform(second_key, (NX, NY, NZ), minval=math.log(0.02), maxval=math.log(0.1))
    base_values = jnp.exp(logs)
    profile = 1.0 + 4.0 * jnp.exp(-((places - center) / spread) ** 2)
    return (base_values * profile[:, None, None]).astype(jnp.float32)


def draw_buildings(key, part):
    first_key, second_key = jax.random.split(key, 2)
    footprint = jax.random.randint(first_key, (NX, NY), 0, 4) == 0
    heights = jax.random.randint(second_key, (NX, NY), 1, NZ // 3 + 1)
    levels = jnp.arange(NZ, dtype=jnp.int32)
    inside = footprint[:, :, None] & (levels[None, None, :] < heights[:, :, None])
    return jnp.where(inside, 1, 0).astype(jnp.int32)


def level_of(stream_key, shape, shards, low, largest):
    def one(dim, parts):
        draws = jax.random.uniform(jax.random.fold_in(jax.random.fold_in(stream_key, 6), dim), (parts,), jnp.float32, low / len(shards), largest / len(shards))
        return jnp.repeat(jnp.exp(draws), shape[dim] // parts).reshape((-1,) + (1,) * (len(shape) - dim - 1))

    factor_of = one(*shards[0])
    for cut in shards[1:]:
        factor_of = factor_of * one(*cut)
    return factor_of


def centred(key, extent, scale, limit, cuts=(), held_as=jnp.bfloat16):
    loudness = level_of(key, extent, cuts, -0.22, 0.18) if cuts else 1.0
    values = jax.random.normal(key, extent, jnp.float32) * scale * loudness
    return jnp.minimum(jnp.maximum(values, -limit), limit).astype(held_as)


def setup_inputs(seed: int = 0, part: int = 0) -> dict:
    arg_keys = jax.random.split(jax.random.key(seed), 7)
    part_splits = jax.random.split(jax.random.fold_in(arg_keys[6], part), 7)
    initial = jnp.clip(jnp.exp(math.log(2.0) - 2.9957323 * jax.random.uniform(part_splits[0], (BLOCKS, NX, NY, NZ), jnp.float32) ** level_of(part_splits[0], (BLOCKS, NX, NY, NZ), ((0, 2), (1, 8)), -0.2, 0.2)), 0.1, 2.0)
    source = jnp.clip(jnp.exp(math.log(1.0) - 2.9996462 * jax.random.uniform(part_splits[1], (BLOCKS, NX, NY, NZ), jnp.float32) ** level_of(part_splits[1], (BLOCKS, NX, NY, NZ), ((0, 2), (1, 8)), -0.2, 0.2)), 0.049804688, 1.0).astype(jnp.bfloat16)
    diffusion = draw_diffusion(jax.random.fold_in(arg_keys[6], 71), part)
    wind_field = centred(arg_keys[3], (3, NX, NY, NZ), 0.15, 0.6, ((1, 8),), jnp.float32)
    buildings = draw_buildings(jax.random.fold_in(arg_keys[6], 71), part)
    strength = jnp.clip(jnp.exp(math.log(2.0) - 1.3862944 * jax.random.uniform(arg_keys[5], (BLOCKS, FINE), jnp.float32) ** level_of(arg_keys[5], (BLOCKS, FINE), ((0, 2),), -0.2, 0.2)), 0.5, 2.0)
    return {"initial": initial, "source": source, "diffusion": diffusion, "wind_field": wind_field, "buildings": buildings, "strength": strength}


lower_bound = 0.5

def ahead(values, direction):
    length = values.shape[direction]
    tail = lax.slice_in_dim(values, 1, length, axis=direction)
    blank = jnp.zeros_like(lax.slice_in_dim(values, 0, 1, axis=direction))
    return jnp.concatenate([tail, blank], axis=direction)

def behind(values, direction):
    length = values.shape[direction]
    head = lax.slice_in_dim(values, 0, length - 1, axis=direction)
    blank = jnp.zeros_like(lax.slice_in_dim(values, 0, 1, axis=direction))
    return jnp.concatenate([blank, head], axis=direction)

def face_terms(masked, winds):
    opened = jnp.where(masked > 0.0, 1.0, 0.0).astype(masked.dtype)
    result = []
    for direction in range(3):
        conduct = jnp.sqrt(masked * ahead(masked, direction))
        velocity = 0.5 * (winds[direction] + ahead(winds[direction], direction)) * opened * ahead(opened, direction)
        result.append((conduct, velocity))
    return tuple(result)

def disk_fields(face_set):
    conduct_sum = jnp.zeros_like(face_set[0][0])
    speed_sum = jnp.zeros_like(face_set[0][0])
    for direction in range(3):
        conduct, velocity = face_set[direction]
        speed = jnp.abs(velocity)
        conduct_sum = conduct_sum + conduct + behind(conduct, direction)
        speed_sum = speed_sum + speed + behind(speed, direction)
    return (conduct_sum, speed_sum)

def operate(values, face_set, rate):
    total = values
    for direction in range(3):
        conduct, velocity = face_set[direction]
        neighbor = ahead(values, direction)
        flowing = conduct * (values - neighbor) + rate * (jnp.maximum(velocity, 0.0) * values + jnp.minimum(velocity, 0.0) * neighbor)
        total = total + flowing - behind(flowing, direction)
    return total

def coefficients(bound):
    theta = (bound + lower_bound) * 0.5
    delta = (bound - lower_bound) * 0.5
    sigma = theta / delta
    rho_one = 1.0 / sigma
    rho_two = 1.0 / (2.0 * sigma - rho_one)
    return (theta, delta, rho_one, rho_two)

def implicit(current, forcing, face_set, rate, bound):
    theta, delta, rho_one, rho_two = coefficients(bound)
    residual = current + forcing - operate(current, face_set, rate)
    update = residual / theta
    moved = current + update
    residual = residual - operate(update, face_set, rate)
    update = rho_two * rho_one * update + 2.0 * rho_two / delta * residual
    return moved + update

def reference(initial, source, diffusion, wind_field, buildings, strength):
    opened = (1 - buildings).astype(jnp.float32)
    masked = diffusion * opened
    forcing = source.astype(jnp.float32) * opened[None]
    face_set = face_terms(masked, (wind_field[0], wind_field[1], wind_field[2]))
    conduct_sum, speed_sum = disk_fields(face_set)
    advanced = []
    bounds = []
    for time_block in range(BLOCKS):
        bound_row = [jnp.max(1.0 + 2.0 * conduct_sum + strength[time_block, fine_step] * speed_sum) for fine_step in range(FINE)]
        bounds.append(bound_row)
        current = initial[time_block] * opened
        for fine_step in range(FINE):
            current = implicit(current, forcing[time_block], face_set, strength[time_block, fine_step], bound_row[fine_step])
        advanced.append(current)
    finals = []
    for time_block in range(BLOCKS):
        if time_block == 0:
            current = initial[0] * opened
        else:
            current = advanced[time_block - 1]
        for fine_step in range(FINE - 1):
            current = implicit(current, forcing[time_block], face_set, strength[time_block, fine_step], bounds[time_block][fine_step])
        finals.append(current)
    return (jnp.stack(advanced), jnp.stack(finals))
```

```python
import functools

import jax
import jax.numpy as jnp
from jax import lax
from jax.experimental import pallas as pl
from jax.experimental.pallas import tpu as pltpu
from jax.sharding import PartitionSpec as P

LOWER = 0.5
MESH = pl.DeviceIdType.MESH


def place(index, count):
    if count % 4:
        return index
    return index + ((index // 2) % 2) * (1 - 2 * (index % 2))


def drain(view, sem):
    pltpu.make_async_copy(view, view, sem).wait()


def after(values, axis):
    length = values.shape[axis]
    return pltpu.roll(values, length - 1, axis)


def before(values, axis):
    return pltpu.roll(values, 1, axis)


def kernel(
    slabs, blocks, rows, width, per, groups,
    initial_ref, source_ref, diffusion_ref, wind_ref, buildings_ref, strength_ref,
    advanced_ref, final_ref,
    initial, source, diffusion, wind, buildings,
    sendc, sends, recvc, recvs, raw, states, rates, gath, outs, back,
    load_sem, a2a_sem, rate_sem, gath_sem, halo_send, halo_recv, out_sem,
):
    layers, ny, nz = diffusion.shape
    nx = slabs * layers
    cores = slabs * blocks
    fine = strength_ref.shape[1]
    ext = rows + 2 * width
    space = lax.axis_index("space")
    time = lax.axis_index("tm")
    mine = place(space, slabs) * blocks + time

    def where(core):
        return {"space": place(core // blocks, slabs), "tm": core % blocks}

    loads = [
        pltpu.make_async_copy(a, b, load_sem.at[i])
        for i, (a, b) in enumerate(
            (
                (buildings_ref, buildings),
                (diffusion_ref, diffusion),
                (wind_ref, wind),
                (initial_ref, initial),
                (source_ref, source),
            )
        )
    ]
    for load in loads:
        load.start()
    blank = jnp.zeros((width, nx, nz), jnp.float32)
    for field in range(raw.shape[0]):
        raw[field, 0:width] = blank
        raw[field, width + rows : ext] = blank
    for index in range(states.shape[0]):
        for block in range(blocks):
            states[index, block, 0:width] = blank
            states[index, block, width + rows : ext] = blank
    for k in range(fine):
        rates[time, k] = jnp.full((8, nz), strength_ref[0, k], jnp.float32)

    barrier = pltpu.get_barrier_semaphore()

    def greet(step, _):
        pl.semaphore_signal(barrier, inc=1, device_id=where((mine + step) % cores), device_id_type=MESH)
        return 0

    lax.fori_loop(1, cores, greet, 0)

    def pack(dest, field, array):
        for layer in range(layers):
            if rows % 8 == 0:
                dest[:, field, layer] = array[layer].reshape(cores, rows, nz)
            else:
                for core in range(cores):
                    dest[core, field, layer] = array[layer, core * rows : (core + 1) * rows]

    for load in loads:
        load.wait()
    opened = (1 - buildings[...]).astype(jnp.float32)
    pack(sendc, 0, diffusion[...] * opened)
    for axis in range(3):
        pack(sendc, 1 + axis, wind[axis])
    pack(sends, 0, initial[0] * opened)
    pack(sends, 1, source[0].astype(jnp.float32) * opened)
    pl.semaphore_wait(barrier, cores - 1)

    rate_copy = [
        pltpu.make_async_remote_copy(
            rates.at[time], rates.at[time], rate_sem.at[0], rate_sem.at[1],
            device_id={"tm": (time + 1) % blocks}, device_id_type=MESH,
        )
    ]
    rate_copy[0].start()

    def send_coef(step, _):
        target = (space + step) % slabs
        core = place(target, slabs) * blocks + time
        pltpu.make_async_remote_copy(
            sendc.at[core], recvc.at[space], a2a_sem.at[0], a2a_sem.at[1],
            device_id={"space": target}, device_id_type=MESH,
        ).start()
        return 0

    def send_state(step, _):
        core = (mine + step) % cores
        pltpu.make_async_remote_copy(
            sends.at[core], recvs.at[space * blocks + time], a2a_sem.at[2], a2a_sem.at[3],
            device_id=where(core), device_id_type=MESH,
        ).start()
        return 0

    lax.fori_loop(1, slabs, send_coef, 0)
    lax.fori_loop(1, cores, send_state, 0)
    pltpu.make_async_copy(sendc.at[mine], recvc.at[space], a2a_sem.at[1]).start()
    pltpu.make_async_copy(sends.at[mine], recvs.at[space * blocks + time], a2a_sem.at[3]).start()
    drain(recvc, a2a_sem.at[1])
    drain(recvs, a2a_sem.at[3])

    def turned(array):
        return jnp.swapaxes(array.reshape(nx, rows, nz), 0, 1)

    inside = slice(width, width + rows)
    for field in range(4):
        raw[field, inside] = turned(recvc[:, field])
    for block in range(blocks):
        for kind in range(2):
            chunk = jnp.stack([recvs[s * blocks + block, kind] for s in range(slabs)])
            raw[4 + kind * blocks + block, inside] = turned(chunk)

    last = cores - 1

    def swap(index, up_source, up_target, down_source, down_target):
        @pl.when(mine < last)
        def _():
            pltpu.make_async_remote_copy(
                up_source, up_target, halo_send.at[index, 0], halo_recv.at[index, 0],
                device_id=where(mine + 1), device_id_type=MESH,
            ).start()

        @pl.when(mine > 0)
        def _():
            pltpu.make_async_remote_copy(
                down_source, down_target, halo_send.at[index, 1], halo_recv.at[index, 1],
                device_id=where(mine - 1), device_id_type=MESH,
            ).start()

    def arrived(index, low, high):
        @pl.when(mine > 0)
        def _():
            drain(low, halo_recv.at[index, 0])

        @pl.when(mine < last)
        def _():
            drain(high, halo_recv.at[index, 1])

    def sent(index, low, high):
        @pl.when(mine < last)
        def _():
            drain(low, halo_send.at[index, 0])

        @pl.when(mine > 0)
        def _():
            drain(high, halo_send.at[index, 1])

    def views(ref):
        return (
            ref.at[:, rows : rows + width],
            ref.at[:, 0:width],
            ref.at[:, width : 2 * width],
            ref.at[:, width + rows : ext],
        )

    swap(0, *views(raw))
    raw_views = views(raw)
    arrived(0, raw_views[1], raw_views[3])
    for copy in rate_copy:
        copy.wait()

    masked = raw[0]
    core_open = jnp.where(masked > 0.0, 1.0, 0.0)
    level = lax.broadcasted_iota(jnp.int32, (ext, nx, nz), 1)
    lane = lax.broadcasted_iota(jnp.int32, (ext, nx, nz), 2)
    wind_x, wind_y, wind_z = raw[1], raw[2], raw[3]

    def face(cut, wind_here, wind_next, masked_next, open_next, masked_here, open_here):
        conduct = jnp.sqrt(masked_here * masked_next)
        velocity = 0.5 * (wind_here + wind_next) * open_here * open_next
        if cut is not None:
            conduct = jnp.where(cut, conduct, 0.0)
            velocity = jnp.where(cut, velocity, 0.0)
        return conduct, velocity

    conduct_x, speed_x = face(
        level < nx - 1, wind_x, after(wind_x, 1), after(masked, 1), after(core_open, 1), masked, core_open
    )
    conduct_z, speed_z = face(
        lane < nz - 1, wind_z, after(wind_z, 2), after(masked, 2), after(core_open, 2), masked, core_open
    )
    conduct_y, speed_y = face(
        None, wind_y[:-1], wind_y[1:], masked[1:], core_open[1:], masked[:-1], core_open[:-1]
    )
    mid = slice(1, ext - 1)
    parts = []
    for conduct, speed, axis in ((conduct_x, speed_x, 1), (conduct_z, speed_z, 2)):
        plus = jnp.maximum(speed, 0.0)
        minus = jnp.maximum(-speed, 0.0)
        parts.append(
            (conduct[mid], minus[mid], before(conduct, axis)[mid], before(plus, axis)[mid],
             plus[mid], before(minus, axis)[mid])
        )
    plus = jnp.maximum(speed_y, 0.0)
    minus = jnp.maximum(-speed_y, 0.0)
    parts.append((conduct_y[1:], minus[1:], conduct_y[:-1], plus[:-1], plus[1:], minus[:-1]))
    conduct_sum = sum(p[0] + p[2] for p in parts)
    flow_sum = sum(p[4] + p[5] for p in parts)
    speed_sum = sum(p[1] + p[3] for p in parts) + flow_sum

    own = slice(width - 1, width - 1 + rows)
    for block in range(blocks):
        for k in range(fine):
            rate = rates[block, k, 0:1]
            bound = 1.0 + 2.0 * conduct_sum[own] + rate * speed_sum[own]
            bound = jnp.max(jnp.max(bound, axis=0), axis=0, keepdims=True)
            j = block * fine + k
            gath[mine, j : j + 1] = bound

    def send_bound(step, _):
        pltpu.make_async_remote_copy(
            gath.at[mine], gath.at[mine], gath_sem.at[0], gath_sem.at[1],
            device_id=where((mine + step) % cores), device_id_type=MESH,
        ).start()
        return 0

    lax.fori_loop(1, cores, send_bound, 0)

    def stencil(values, faces, axis_shift):
        inner = values[1:-1]
        first, second, third = faces
        total = first[0] * after(inner, 1) + first[1] * before(inner, 1)
        total = total + second[0] * after(inner, 2) + second[1] * before(inner, 2)
        return total + third[0] * values[2:] + third[1] * values[:-2]

    weights = []

    def weight_rows():
        if not weights:
            drain(gath.at[0 : cores - 1], gath_sem.at[1])
            bound = jnp.max(jnp.max(gath[...], axis=0), axis=1, keepdims=True)
            bound = jnp.broadcast_to(bound, (gath.shape[1], nz))
            theta = (bound + LOWER) * 0.5
            delta = (bound - LOWER) * 0.5
            sigma = theta / delta
            rho_one = 1.0 / sigma
            rho_two = 1.0 / (2.0 * sigma - rho_one)
            beta = 2.0 * rho_two / (delta * theta)
            weights.append((1.0 + rho_two * rho_one) / theta + 2.0 * rho_two / delta)
            weights.append(beta)
        return weights

    def advance(values, off, block, k):
        count = ext - 2 * off
        rate = rates[block, k, 0:1]
        reach = slice(off, off + count - 2)
        faces = [(p[0][reach] + rate * p[1][reach], p[2][reach] + rate * p[3][reach]) for p in parts]
        diagonal = conduct_sum[reach] + rate * flow_sum[reach]
        forcing = raw[4 + blocks + block, off + 1 : off + count - 1]
        residual = forcing - diagonal * values[1:-1] + stencil(values, faces, 0)
        narrow = [(a[1:-1], b[1:-1]) for a, b in faces]
        inner = residual[1:-1]
        applied = inner + diagonal[1:-1] * inner - stencil(residual, narrow, 0)
        alpha, beta = weight_rows()
        j = block * fine + k
        return values[2:-2] + alpha[j : j + 1] * inner - beta[j : j + 1] * applied

    def deliver(slot, owner_block, value):
        outs[slot] = jnp.swapaxes(value, 0, 1).reshape(slabs, layers, rows, nz)
        kind = slot // blocks

        def send(step, _):
            target = (space + step) % slabs
            pltpu.make_async_remote_copy(
                outs.at[slot, target], back.at[kind, mine], out_sem.at[slot], out_sem.at[2 * blocks + kind],
                device_id={"space": target, "tm": owner_block}, device_id_type=MESH,
            ).start()
            return 0

        lax.fori_loop(1, slabs, send, 0)

        @pl.when(time == owner_block)
        def _():
            pltpu.make_async_copy(
                outs.at[slot, space], back.at[kind, mine], out_sem.at[2 * blocks + kind]
            ).start()

        @pl.when(time != owner_block)
        def _():
            pltpu.make_async_remote_copy(
                outs.at[slot, space], back.at[kind, mine], out_sem.at[slot], out_sem.at[2 * blocks + kind],
                device_id={"tm": owner_block}, device_id_type=MESH,
            ).start()

    def settled(slot, owner_block):
        drain(outs.at[slot, 0 : slabs - 1], out_sem.at[slot])

        @pl.when(time != owner_block)
        def _():
            drain(outs.at[slot, 0], out_sem.at[slot])

    def trim(values, off):
        low = width - off
        return values[low : low + rows]

    exchange = 0
    current = [raw[4 + block] for block in range(blocks)]
    off = 0
    live = list(range(blocks))
    exchanges = []
    for step in range(2 * fine - 1):
        second = step >= fine
        k = step - fine if second else step
        if step == fine:
            live = [blocks - 1]
        if step and (off + 2 > width):
            for block in live:
                states[exchange, block, inside] = trim(current[block], off)
            part = states.at[exchange, live[0] : live[-1] + 1]
            cuts = (
                part.at[:, rows : rows + width], part.at[:, 0:width],
                part.at[:, width : 2 * width], part.at[:, width + rows : ext],
            )
            swap(exchange + 1, *cuts)
            arrived(exchange + 1, cuts[1], cuts[3])
            exchanges.append((exchange + 1, cuts))
            for block in live:
                current[block] = states[exchange, block]
            off = 0
            exchange += 1
        for block in live:
            current[block] = advance(current[block], off, block, k)
        off += 2
        if step == fine - 2:
            deliver(blocks, 0, trim(current[0], off))
        if step == fine - 1:
            for block in range(blocks):
                deliver(block, block, trim(current[block], off))
            current[1] = current[0]
    deliver(blocks + 1, 1, trim(current[1], off))

    def unpack(dest, kind):
        for layer in range(layers):
            if rows % 8 == 0:
                dest[0, layer] = back[kind, :, layer].reshape(ny, nz)
            else:
                for core in range(cores):
                    dest[0, layer, core * rows : (core + 1) * rows] = back[kind, core, layer]

    drain(back.at[0], out_sem.at[2 * blocks])
    unpack(advanced_ref, 0)
    sent(0, raw_views[0], raw_views[2])
    for index, cuts in exchanges:
        sent(index, cuts[0], cuts[2])
    drain(recvc.at[0 : slabs - 1], a2a_sem.at[0])
    drain(recvs.at[0 : cores - 1], a2a_sem.at[2])
    drain(gath.at[0 : cores - 1], gath_sem.at[0])
    for kind in range(2):
        for block in range(blocks):
            settled(kind * blocks + block, block)
    drain(back.at[1], out_sem.at[2 * blocks + 1])
    unpack(final_ref, 1)


def solution(mesh):
    slabs = mesh.shape["space"]
    blocks = mesh.shape["tm"]

    def shards(initial, source, diffusion, wind_field, buildings, strength):
        layers, ny, nz = diffusion.shape
        nx = layers * slabs
        cores = slabs * blocks
        rows = ny // cores
        fine = strength.shape[1]
        width = 4 if rows >= 4 else 2
        per = width // 2
        groups = -(-(2 * fine - 1) // per) - 1
        ext = rows + 2 * width
        f32 = jnp.float32
        return pl.pallas_call(
            functools.partial(kernel, slabs, blocks, rows, width, per, groups),
            out_shape=[jax.ShapeDtypeStruct(initial.shape, f32)] * 2,
            in_specs=[pl.BlockSpec(memory_space=pl.ANY)] * 5 + [pl.BlockSpec(memory_space=pltpu.SMEM)],
            out_specs=[pl.BlockSpec(memory_space=pltpu.VMEM)] * 2,
            scratch_shapes=[
                pltpu.VMEM(initial.shape, f32),
                pltpu.VMEM(source.shape, source.dtype),
                pltpu.VMEM(diffusion.shape, f32),
                pltpu.VMEM(wind_field.shape, f32),
                pltpu.VMEM(buildings.shape, buildings.dtype),
                pltpu.VMEM((cores, 4, layers, rows, nz), f32),
                pltpu.VMEM((cores, 2, layers, rows, nz), f32),
                pltpu.VMEM((slabs, 4, layers, rows, nz), f32),
                pltpu.VMEM((cores, 2, layers, rows, nz), f32),
                pltpu.VMEM((4 + 2 * blocks, ext, nx, nz), f32),
                pltpu.VMEM((groups, blocks, ext, nx, nz), f32),
                pltpu.VMEM((blocks, fine, 8, nz), f32),
                pltpu.VMEM((cores, blocks * fine, nz), f32),
                pltpu.VMEM((2 * blocks, slabs, layers, rows, nz), f32),
                pltpu.VMEM((2, cores, layers, rows, nz), f32),
                pltpu.SemaphoreType.DMA((5,)),
                pltpu.SemaphoreType.DMA((4,)),
                pltpu.SemaphoreType.DMA((2,)),
                pltpu.SemaphoreType.DMA((2,)),
                pltpu.SemaphoreType.DMA((groups + 1, 2)),
                pltpu.SemaphoreType.DMA((groups + 1, 2)),
                pltpu.SemaphoreType.DMA((2 * blocks + 2,)),
            ],
            compiler_params=pltpu.CompilerParams(
                collective_id=0, has_side_effects=True, vmem_limit_bytes=48 << 20
            ),
        )(initial, source, diffusion, wind_field, buildings, strength)

    in_specs = (
        P(("copy", "tm"), "space", None, None),
        P(("copy", "tm"), "space", None, None),
        P("space", None, None),
        P(None, "space", None, None),
        P("space", None, None),
        P("tm", None),
    )
    out_specs = (P(("copy", "tm"), "space", None, None), P(("copy", "tm"), "space", None, None))
    return jax.shard_map(shards, mesh=mesh, in_specs=in_specs, out_specs=out_specs, check_vma=False)
```

```python
import functools

import jax
import jax.numpy as jnp
from jax import lax
from jax.experimental import pallas as pl
from jax.experimental.pallas import tpu as pltpu
from jax.sharding import PartitionSpec as P

LOWER = 0.5
MESH = pl.DeviceIdType.MESH


def place(index, count):
    if count % 4:
        return index
    return index + ((index // 2) % 2) * (1 - 2 * (index % 2))


def drain(view, sem):
    pltpu.make_async_copy(view, view, sem).wait()


def after(values, axis):
    length = values.shape[axis]
    return pltpu.roll(values, length - 1, axis)


def before(values, axis):
    return pltpu.roll(values, 1, axis)


def kernel(
    slabs, blocks, rows, width, per, groups,
    initial_ref, source_ref, diffusion_ref, wind_ref, buildings_ref, strength_ref,
    advanced_ref, final_ref,
    initial, source, diffusion, wind, buildings,
    sendc, sends, recvc, recvs, raw, states, rates, gath, outs, back,
    load_sem, a2a_sem, rate_sem, gath_sem, halo_send, halo_recv, out_sem,
):
    layers, ny, nz = diffusion.shape
    nx = slabs * layers
    cores = slabs * blocks
    fine = strength_ref.shape[1]
    ext = rows + 2 * width
    space = lax.axis_index("space")
    time = lax.axis_index("tm")
    mine = place(space, slabs) * blocks + time

    def where(core):
        return {"space": place(core // blocks, slabs), "tm": core % blocks}

    loads = [
        pltpu.make_async_copy(a, b, load_sem.at[i])
        for i, (a, b) in enumerate(
            (
                (buildings_ref, buildings),
                (diffusion_ref, diffusion),
                (wind_ref, wind),
                (initial_ref, initial),
                (source_ref, source),
            )
        )
    ]
    for load in loads:
        load.start()
    blank = jnp.zeros((width, nx, nz), jnp.float32)
    for field in range(raw.shape[0]):
        raw[field, 0:width] = blank
        raw[field, width + rows : ext] = blank
    for index in range(states.shape[0]):
        for block in range(blocks):
            states[index, block, 0:width] = blank
            states[index, block, width + rows : ext] = blank
    for k in range(fine):
        rates[time, k] = jnp.full((8, nz), strength_ref[0, k], jnp.float32)

    barrier = pltpu.get_barrier_semaphore()

    def greet(step, _):
        pl.semaphore_signal(barrier, inc=1, device_id=where((mine + step) % cores), device_id_type=MESH)
        return 0

    lax.fori_loop(1, cores, greet, 0)

    def pack(dest, field, array):
        for layer in range(layers):
            if rows % 8 == 0:
                dest[:, field, layer] = array[layer].reshape(cores, rows, nz)
            else:
                for core in range(cores):
                    dest[core, field, layer] = array[layer, core * rows : (core + 1) * rows]

    for load in loads:
        load.wait()
    opened = (1 - buildings[...]).astype(jnp.float32)
    pack(sendc, 0, diffusion[...] * opened)
    for axis in range(3):
        pack(sendc, 1 + axis, wind[axis])
    pack(sends, 0, initial[0] * opened)
    pack(sends, 1, source[0].astype(jnp.float32) * opened)
    pl.semaphore_wait(barrier, cores - 1)

    rate_copy = [
        pltpu.make_async_remote_copy(
            rates.at[time], rates.at[time], rate_sem.at[0], rate_sem.at[1],
            device_id={"tm": (time + 1) % blocks}, device_id_type=MESH,
        )
    ]
    rate_copy[0].start()

    def send_coef(step, _):
        target = (space + step) % slabs
        core = place(target, slabs) * blocks + time
        pltpu.make_async_remote_copy(
            sendc.at[core], recvc.at[space], a2a_sem.at[0], a2a_sem.at[1],
            device_id={"space": target}, device_id_type=MESH,
        ).start()
        return 0

    def send_state(step, _):
        core = (mine + step) % cores
        pltpu.make_async_remote_copy(
            sends.at[core], recvs.at[space * blocks + time], a2a_sem.at[2], a2a_sem.at[3],
            device_id=where(core), device_id_type=MESH,
        ).start()
        return 0

    lax.fori_loop(1, slabs, send_coef, 0)
    lax.fori_loop(1, cores, send_state, 0)
    pltpu.make_async_copy(sendc.at[mine], recvc.at[space], a2a_sem.at[1]).start()
    pltpu.make_async_copy(sends.at[mine], recvs.at[space * blocks + time], a2a_sem.at[3]).start()

    def turned(array):
        return jnp.swapaxes(array.reshape(nx, rows, nz), 0, 1)

    inside = slice(width, width + rows)
    last = cores - 1

    def swap(index, up_source, up_target, down_source, down_target):
        @pl.when(mine < last)
        def _():
            pltpu.make_async_remote_copy(
                up_source, up_target, halo_send.at[index, 0], halo_recv.at[index, 0],
                device_id=where(mine + 1), device_id_type=MESH,
            ).start()

        @pl.when(mine > 0)
        def _():
            pltpu.make_async_remote_copy(
                down_source, down_target, halo_send.at[index, 1], halo_recv.at[index, 1],
                device_id=where(mine - 1), device_id_type=MESH,
            ).start()

    def arrived(index, low, high):
        @pl.when(mine > 0)
        def _():
            drain(low, halo_recv.at[index, 0])

        @pl.when(mine < last)
        def _():
            drain(high, halo_recv.at[index, 1])

    def sent(index, low, high):
        @pl.when(mine < last)
        def _():
            drain(low, halo_send.at[index, 0])

        @pl.when(mine > 0)
        def _():
            drain(high, halo_send.at[index, 1])

    def views(ref):
        return (
            ref.at[:, rows : rows + width],
            ref.at[:, 0:width],
            ref.at[:, width : 2 * width],
            ref.at[:, width + rows : ext],
        )

    drain(recvc, a2a_sem.at[1])
    for field in range(4):
        raw[field, inside] = turned(recvc[:, field])
    coef_views = views(raw.at[0:4])
    swap(0, *coef_views)
    for copy in rate_copy:
        copy.wait()
    arrived(0, coef_views[1], coef_views[3])

    masked = raw[0]
    core_open = jnp.where(masked > 0.0, 1.0, 0.0)
    level = lax.broadcasted_iota(jnp.int32, (ext, nx, nz), 1)
    lane = lax.broadcasted_iota(jnp.int32, (ext, nx, nz), 2)
    wind_x, wind_y, wind_z = raw[1], raw[2], raw[3]

    def face(cut, wind_here, wind_next, masked_next, open_next, masked_here, open_here):
        conduct = jnp.sqrt(masked_here * masked_next)
        velocity = 0.5 * (wind_here + wind_next) * open_here * open_next
        if cut is not None:
            conduct = jnp.where(cut, conduct, 0.0)
            velocity = jnp.where(cut, velocity, 0.0)
        return conduct, velocity

    conduct_x, speed_x = face(
        level < nx - 1, wind_x, after(wind_x, 1), after(masked, 1), after(core_open, 1), masked, core_open
    )
    conduct_z, speed_z = face(
        lane < nz - 1, wind_z, after(wind_z, 2), after(masked, 2), after(core_open, 2), masked, core_open
    )
    conduct_y, speed_y = face(
        None, wind_y[:-1], wind_y[1:], masked[1:], core_open[1:], masked[:-1], core_open[:-1]
    )
    mid = slice(1, ext - 1)
    parts = []
    for conduct, speed, axis in ((conduct_x, speed_x, 1), (conduct_z, speed_z, 2)):
        plus = jnp.maximum(speed, 0.0)
        minus = jnp.maximum(-speed, 0.0)
        parts.append(
            (conduct[mid], minus[mid], before(conduct, axis)[mid], before(plus, axis)[mid],
             plus[mid], before(minus, axis)[mid])
        )
    plus = jnp.maximum(speed_y, 0.0)
    minus = jnp.maximum(-speed_y, 0.0)
    parts.append((conduct_y[1:], minus[1:], conduct_y[:-1], plus[:-1], plus[1:], minus[:-1]))
    conduct_sum = sum(p[0] + p[2] for p in parts)
    flow_sum = sum(p[4] + p[5] for p in parts)
    speed_sum = sum(p[1] + p[3] for p in parts) + flow_sum

    own = slice(width - 1, width - 1 + rows)
    for block in range(blocks):
        for k in range(fine):
            rate = rates[block, k, 0:1]
            bound = 1.0 + 2.0 * conduct_sum[own] + rate * speed_sum[own]
            bound = jnp.max(jnp.max(bound, axis=0), axis=0, keepdims=True)
            j = block * fine + k
            gath[mine, j : j + 1] = bound

    def send_bound(step, _):
        pltpu.make_async_remote_copy(
            gath.at[mine], gath.at[mine], gath_sem.at[0], gath_sem.at[1],
            device_id=where((mine + step) % cores), device_id_type=MESH,
        ).start()
        return 0

    lax.fori_loop(1, cores, send_bound, 0)

    drain(recvs, a2a_sem.at[3])
    for block in range(blocks):
        for kind in range(2):
            chunk = jnp.stack([recvs[s * blocks + block, kind] for s in range(slabs)])
            raw[4 + kind * blocks + block, inside] = turned(chunk)
    state_views = views(raw.at[4 : 4 + 2 * blocks])
    swap(1, *state_views)
    arrived(1, state_views[1], state_views[3])

    def stencil(values, faces, axis_shift):
        inner = values[1:-1]
        first, second, third = faces
        total = first[0] * after(inner, 1) + first[1] * before(inner, 1)
        total = total + second[0] * after(inner, 2) + second[1] * before(inner, 2)
        return total + third[0] * values[2:] + third[1] * values[:-2]

    weights = []

    def weight_rows():
        if not weights:
            drain(gath.at[0 : cores - 1], gath_sem.at[1])
            bound = jnp.max(jnp.max(gath[...], axis=0), axis=1, keepdims=True)
            bound = jnp.broadcast_to(bound, (gath.shape[1], nz))
            theta = (bound + LOWER) * 0.5
            delta = (bound - LOWER) * 0.5
            sigma = theta / delta
            rho_one = 1.0 / sigma
            rho_two = 1.0 / (2.0 * sigma - rho_one)
            beta = 2.0 * rho_two / (delta * theta)
            weights.append((1.0 + rho_two * rho_one) / theta + 2.0 * rho_two / delta)
            weights.append(beta)
        return weights

    def advance(values, off, block, k):
        count = ext - 2 * off
        rate = rates[block, k, 0:1]
        reach = slice(off, off + count - 2)
        faces = [(p[0][reach] + rate * p[1][reach], p[2][reach] + rate * p[3][reach]) for p in parts]
        diagonal = conduct_sum[reach] + rate * flow_sum[reach]
        forcing = raw[4 + blocks + block, off + 1 : off + count - 1]
        residual = forcing - diagonal * values[1:-1] + stencil(values, faces, 0)
        narrow = [(a[1:-1], b[1:-1]) for a, b in faces]
        inner = residual[1:-1]
        applied = inner + diagonal[1:-1] * inner - stencil(residual, narrow, 0)
        alpha, beta = weight_rows()
        j = block * fine + k
        return values[2:-2] + alpha[j : j + 1] * inner - beta[j : j + 1] * applied

    def deliver(slot, owner_block, value):
        outs[slot] = jnp.swapaxes(value, 0, 1).reshape(slabs, layers, rows, nz)
        kind = slot // blocks

        def send(step, _):
            target = (space + step) % slabs
            pltpu.make_async_remote_copy(
                outs.at[slot, target], back.at[kind, mine], out_sem.at[slot], out_sem.at[2 * blocks + kind],
                device_id={"space": target, "tm": owner_block}, device_id_type=MESH,
            ).start()
            return 0

        lax.fori_loop(1, slabs, send, 0)

        @pl.when(time == owner_block)
        def _():
            pltpu.make_async_copy(
                outs.at[slot, space], back.at[kind, mine], out_sem.at[2 * blocks + kind]
            ).start()

        @pl.when(time != owner_block)
        def _():
            pltpu.make_async_remote_copy(
                outs.at[slot, space], back.at[kind, mine], out_sem.at[slot], out_sem.at[2 * blocks + kind],
                device_id={"tm": owner_block}, device_id_type=MESH,
            ).start()

    def settled(slot, owner_block):
        drain(outs.at[slot, 0 : slabs - 1], out_sem.at[slot])

        @pl.when(time != owner_block)
        def _():
            drain(outs.at[slot, 0], out_sem.at[slot])

    def trim(values, off):
        low = width - off
        return values[low : low + rows]

    exchange = 0
    current = [raw[4 + block] for block in range(blocks)]
    off = 0
    live = list(range(blocks))
    exchanges = []
    for step in range(2 * fine - 1):
        second = step >= fine
        k = step - fine if second else step
        if step == fine:
            live = [blocks - 1]
        if step and (off + 2 > width):
            for block in live:
                states[exchange, block, inside] = trim(current[block], off)
            part = states.at[exchange, live[0] : live[-1] + 1]
            cuts = (
                part.at[:, rows : rows + width], part.at[:, 0:width],
                part.at[:, width : 2 * width], part.at[:, width + rows : ext],
            )
            swap(exchange + 2, *cuts)
            arrived(exchange + 2, cuts[1], cuts[3])
            exchanges.append((exchange + 2, cuts))
            for block in live:
                current[block] = states[exchange, block]
            off = 0
            exchange += 1
        for block in live:
            current[block] = advance(current[block], off, block, k)
        off += 2
        if step == fine - 2:
            deliver(blocks, 0, trim(current[0], off))
        if step == fine - 1:
            for block in range(blocks):
                deliver(block, block, trim(current[block], off))
            current[1] = current[0]
    deliver(blocks + 1, 1, trim(current[1], off))

    def unpack(dest, kind):
        for layer in range(layers):
            if rows % 8 == 0:
                dest[0, layer] = back[kind, :, layer].reshape(ny, nz)
            else:
                for core in range(cores):
                    dest[0, layer, core * rows : (core + 1) * rows] = back[kind, core, layer]

    drain(back.at[0], out_sem.at[2 * blocks])
    unpack(advanced_ref, 0)
    sent(0, coef_views[0], coef_views[2])
    sent(1, state_views[0], state_views[2])
    for index, cuts in exchanges:
        sent(index, cuts[0], cuts[2])
    drain(recvc.at[0 : slabs - 1], a2a_sem.at[0])
    drain(recvs.at[0 : cores - 1], a2a_sem.at[2])
    drain(gath.at[0 : cores - 1], gath_sem.at[0])
    for kind in range(2):
        for block in range(blocks):
            settled(kind * blocks + block, block)
    drain(back.at[1], out_sem.at[2 * blocks + 1])
    unpack(final_ref, 1)


def solution(mesh):
    slabs = mesh.shape["space"]
    blocks = mesh.shape["tm"]

    def shards(initial, source, diffusion, wind_field, buildings, strength):
        layers, ny, nz = diffusion.shape
        nx = layers * slabs
        cores = slabs * blocks
        rows = ny // cores
        fine = strength.shape[1]
        width = 8 if rows >= 8 else 2
        per = width // 2
        groups = -(-(2 * fine - 1) // per) - 1
        ext = rows + 2 * width
        f32 = jnp.float32
        return pl.pallas_call(
            functools.partial(kernel, slabs, blocks, rows, width, per, groups),
            out_shape=[jax.ShapeDtypeStruct(initial.shape, f32)] * 2,
            in_specs=[pl.BlockSpec(memory_space=pltpu.HBM)] * 5 + [pl.BlockSpec(memory_space=pltpu.SMEM)],
            out_specs=[pl.BlockSpec(memory_space=pltpu.VMEM)] * 2,
            scratch_shapes=[
                pltpu.VMEM(initial.shape, f32),
                pltpu.VMEM(source.shape, source.dtype),
                pltpu.VMEM(diffusion.shape, f32),
                pltpu.VMEM(wind_field.shape, f32),
                pltpu.VMEM(buildings.shape, buildings.dtype),
                pltpu.VMEM((cores, 4, layers, rows, nz), f32),
                pltpu.VMEM((cores, 2, layers, rows, nz), f32),
                pltpu.VMEM((slabs, 4, layers, rows, nz), f32),
                pltpu.VMEM((cores, 2, layers, rows, nz), f32),
                pltpu.VMEM((4 + 2 * blocks, ext, nx, nz), f32),
                pltpu.VMEM((groups, blocks, ext, nx, nz), f32),
                pltpu.VMEM((blocks, fine, 8, nz), f32),
                pltpu.VMEM((cores, blocks * fine, nz), f32),
                pltpu.VMEM((2 * blocks, slabs, layers, rows, nz), f32),
                pltpu.VMEM((2, cores, layers, rows, nz), f32),
                pltpu.SemaphoreType.DMA((5,)),
                pltpu.SemaphoreType.DMA((4,)),
                pltpu.SemaphoreType.DMA((2,)),
                pltpu.SemaphoreType.DMA((2,)),
                pltpu.SemaphoreType.DMA((groups + 2, 2)),
                pltpu.SemaphoreType.DMA((groups + 2, 2)),
                pltpu.SemaphoreType.DMA((2 * blocks + 2,)),
            ],
            compiler_params=pltpu.CompilerParams(
                collective_id=0, has_side_effects=True, vmem_limit_bytes=63 << 20
            ),
        )(initial, source, diffusion, wind_field, buildings, strength)

    in_specs = (
        P(("copy", "tm"), "space", None, None),
        P(("copy", "tm"), "space", None, None),
        P("space", None, None),
        P(None, "space", None, None),
        P("space", None, None),
        P("tm", None),
    )
    out_specs = (P(("copy", "tm"), "space", None, None), P(("copy", "tm"), "space", None, None))
    return jax.shard_map(shards, mesh=mesh, in_specs=in_specs, out_specs=out_specs, check_vma=False)
```

```python
import functools

import jax
import jax.numpy as jnp
from jax import lax
from jax.experimental import pallas as pl
from jax.experimental.pallas import tpu as pltpu
from jax.sharding import PartitionSpec as P

LOWER = 0.5
MESH = pl.DeviceIdType.MESH


def place(index, count):
    if count % 4:
        return index
    return index + ((index // 2) % 2) * (1 - 2 * (index % 2))


def drain(view, sem):
    pltpu.make_async_copy(view, view, sem).wait()


def after(values, axis):
    length = values.shape[axis]
    return pltpu.roll(values, length - 1, axis)


def before(values, axis):
    return pltpu.roll(values, 1, axis)


def kernel(
    slabs, blocks, rows, width, per, groups,
    initial_ref, source_ref, diffusion_ref, wind_ref, buildings_ref, strength_ref,
    advanced_ref, final_ref,
    initial, source, diffusion, wind, buildings, strength,
    sendc, sends, recvc, recvs, raw, states, rates, gath, outs, back,
    load_sem, a2a_sem, rate_sem, gath_sem, halo_send, halo_recv, out_sem,
):
    layers, ny, nz = diffusion.shape
    nx = slabs * layers
    cores = slabs * blocks
    fine = strength_ref.shape[1]
    ext = rows + 2 * width
    space = lax.axis_index("space")
    time = lax.axis_index("tm")
    mine = place(space, slabs) * blocks + time

    def where(core):
        return {"space": place(core // blocks, slabs), "tm": core % blocks}

    loads = [
        pltpu.make_async_copy(a, b, load_sem.at[i])
        for i, (a, b) in enumerate(
            (
                (buildings_ref, buildings),
                (diffusion_ref, diffusion),
                (wind_ref, wind),
                (initial_ref, initial),
                (source_ref, source),
                (strength_ref, strength),
            )
        )
    ]
    for load in loads:
        load.start()
    blank = jnp.zeros((width, nx, nz), jnp.float32)
    for field in range(raw.shape[0]):
        raw[field, 0:width] = blank
        raw[field, width + rows : ext] = blank
    for index in range(states.shape[0]):
        for block in range(blocks):
            states[index, block, 0:width] = blank
            states[index, block, width + rows : ext] = blank

    barrier = pltpu.get_barrier_semaphore()

    def greet(step, _):
        pl.semaphore_signal(barrier, inc=1, device_id=where((mine + step) % cores), device_id_type=MESH)
        return 0

    lax.fori_loop(1, cores, greet, 0)

    def pack(dest, field, array):
        for layer in range(layers):
            if rows % 8 == 0:
                dest[:, field, layer] = array[layer].reshape(cores, rows, nz)
            else:
                for core in range(cores):
                    dest[core, field, layer] = array[layer, core * rows : (core + 1) * rows]

    for load in loads:
        load.wait()
    for k in range(fine):
        rates[time, k] = jnp.broadcast_to(strength[0:1, k : k + 1], (8, nz))
    opened = (1 - buildings[...]).astype(jnp.float32)
    pack(sendc, 0, diffusion[...] * opened)
    for axis in range(3):
        pack(sendc, 1 + axis, wind[axis])
    pack(sends, 0, initial[0] * opened)
    pack(sends, 1, source[0].astype(jnp.float32) * opened)
    pl.semaphore_wait(barrier, cores - 1)

    rate_copy = [
        pltpu.make_async_remote_copy(
            rates.at[time], rates.at[time], rate_sem.at[0], rate_sem.at[1],
            device_id={"tm": (time + 1) % blocks}, device_id_type=MESH,
        )
    ]
    rate_copy[0].start()

    def send_coef(step, _):
        target = (space + step) % slabs
        core = place(target, slabs) * blocks + time
        pltpu.make_async_remote_copy(
            sendc.at[core], recvc.at[space], a2a_sem.at[0], a2a_sem.at[1],
            device_id={"space": target}, device_id_type=MESH,
        ).start()
        return 0

    def send_state(step, _):
        core = (mine + step) % cores
        pltpu.make_async_remote_copy(
            sends.at[core], recvs.at[space * blocks + time], a2a_sem.at[2], a2a_sem.at[3],
            device_id=where(core), device_id_type=MESH,
        ).start()
        return 0

    lax.fori_loop(1, slabs, send_coef, 0)
    lax.fori_loop(1, cores, send_state, 0)
    pltpu.make_async_copy(sendc.at[mine], recvc.at[space], a2a_sem.at[1]).start()
    pltpu.make_async_copy(sends.at[mine], recvs.at[space * blocks + time], a2a_sem.at[3]).start()

    def turned(array):
        return jnp.swapaxes(array.reshape(nx, rows, nz), 0, 1)

    inside = slice(width, width + rows)
    last = cores - 1

    def swap(index, up_source, up_target, down_source, down_target):
        @pl.when(mine < last)
        def _():
            pltpu.make_async_remote_copy(
                up_source, up_target, halo_send.at[index, 0], halo_recv.at[index, 0],
                device_id=where(mine + 1), device_id_type=MESH,
            ).start()

        @pl.when(mine > 0)
        def _():
            pltpu.make_async_remote_copy(
                down_source, down_target, halo_send.at[index, 1], halo_recv.at[index, 1],
                device_id=where(mine - 1), device_id_type=MESH,
            ).start()

    def arrived(index, low, high):
        @pl.when(mine > 0)
        def _():
            drain(low, halo_recv.at[index, 0])

        @pl.when(mine < last)
        def _():
            drain(high, halo_recv.at[index, 1])

    def sent(index, low, high):
        @pl.when(mine < last)
        def _():
            drain(low, halo_send.at[index, 0])

        @pl.when(mine > 0)
        def _():
            drain(high, halo_send.at[index, 1])

    def views(ref):
        return (
            ref.at[:, rows : rows + width],
            ref.at[:, 0:width],
            ref.at[:, width : 2 * width],
            ref.at[:, width + rows : ext],
        )

    drain(recvc, a2a_sem.at[1])
    for field in range(4):
        raw[field, inside] = turned(recvc[:, field])
    coef_views = views(raw.at[0:4])
    swap(0, *coef_views)
    for copy in rate_copy:
        copy.wait()
    arrived(0, coef_views[1], coef_views[3])

    masked = raw[0]
    core_open = jnp.where(masked > 0.0, 1.0, 0.0)
    level = lax.broadcasted_iota(jnp.int32, (ext, nx, nz), 1)
    lane = lax.broadcasted_iota(jnp.int32, (ext, nx, nz), 2)
    wind_x, wind_y, wind_z = raw[1], raw[2], raw[3]

    def face(cut, wind_here, wind_next, masked_next, open_next, masked_here, open_here):
        conduct = jnp.sqrt(masked_here * masked_next)
        velocity = 0.5 * (wind_here + wind_next) * open_here * open_next
        if cut is not None:
            conduct = jnp.where(cut, conduct, 0.0)
            velocity = jnp.where(cut, velocity, 0.0)
        return conduct, velocity

    conduct_x, speed_x = face(
        level < nx - 1, wind_x, after(wind_x, 1), after(masked, 1), after(core_open, 1), masked, core_open
    )
    conduct_z, speed_z = face(
        lane < nz - 1, wind_z, after(wind_z, 2), after(masked, 2), after(core_open, 2), masked, core_open
    )
    conduct_y, speed_y = face(
        None, wind_y[:-1], wind_y[1:], masked[1:], core_open[1:], masked[:-1], core_open[:-1]
    )
    mid = slice(1, ext - 1)
    parts = []
    for conduct, speed, axis in ((conduct_x, speed_x, 1), (conduct_z, speed_z, 2)):
        plus = jnp.maximum(speed, 0.0)
        minus = jnp.maximum(-speed, 0.0)
        parts.append(
            (conduct[mid], minus[mid], before(conduct, axis)[mid], before(plus, axis)[mid],
             plus[mid], before(minus, axis)[mid])
        )
    plus = jnp.maximum(speed_y, 0.0)
    minus = jnp.maximum(-speed_y, 0.0)
    parts.append((conduct_y[1:], minus[1:], conduct_y[:-1], plus[:-1], plus[1:], minus[:-1]))
    conduct_sum = sum(p[0] + p[2] for p in parts)
    flow_sum = sum(p[4] + p[5] for p in parts)
    speed_sum = sum(p[1] + p[3] for p in parts) + flow_sum

    own = slice(width - 1, width - 1 + rows)
    for block in range(blocks):
        for k in range(fine):
            rate = rates[block, k, 0:1]
            bound = 1.0 + 2.0 * conduct_sum[own] + rate * speed_sum[own]
            bound = jnp.max(jnp.max(bound, axis=0), axis=0, keepdims=True)
            j = block * fine + k
            gath[mine, j : j + 1] = bound

    def send_bound(step, _):
        pltpu.make_async_remote_copy(
            gath.at[mine], gath.at[mine], gath_sem.at[0], gath_sem.at[1],
            device_id=where((mine + step) % cores), device_id_type=MESH,
        ).start()
        return 0

    lax.fori_loop(1, cores, send_bound, 0)

    drain(recvs, a2a_sem.at[3])
    for block in range(blocks):
        for kind in range(2):
            chunk = jnp.stack([recvs[s * blocks + block, kind] for s in range(slabs)])
            raw[4 + kind * blocks + block, inside] = turned(chunk)
    state_views = views(raw.at[4 : 4 + 2 * blocks])
    swap(1, *state_views)
    arrived(1, state_views[1], state_views[3])

    def stencil(values, faces, axis_shift):
        inner = values[1:-1]
        first, second, third = faces
        total = first[0] * after(inner, 1) + first[1] * before(inner, 1)
        total = total + second[0] * after(inner, 2) + second[1] * before(inner, 2)
        return total + third[0] * values[2:] + third[1] * values[:-2]

    weights = []

    def weight_rows():
        if not weights:
            drain(gath.at[0 : cores - 1], gath_sem.at[1])
            bound = jnp.max(jnp.max(gath[...], axis=0), axis=1, keepdims=True)
            bound = jnp.broadcast_to(bound, (gath.shape[1], nz))
            theta = (bound + LOWER) * 0.5
            delta = (bound - LOWER) * 0.5
            sigma = theta / delta
            rho_one = 1.0 / sigma
            rho_two = 1.0 / (2.0 * sigma - rho_one)
            beta = 2.0 * rho_two / (delta * theta)
            weights.append((1.0 + rho_two * rho_one) / theta + 2.0 * rho_two / delta)
            weights.append(beta)
        return weights

    def advance(values, off, block, k):
        count = ext - 2 * off
        rate = rates[block, k, 0:1]
        reach = slice(off, off + count - 2)
        faces = [(p[0][reach] + rate * p[1][reach], p[2][reach] + rate * p[3][reach]) for p in parts]
        diagonal = conduct_sum[reach] + rate * flow_sum[reach]
        forcing = raw[4 + blocks + block, off + 1 : off + count - 1]
        residual = forcing - diagonal * values[1:-1] + stencil(values, faces, 0)
        narrow = [(a[1:-1], b[1:-1]) for a, b in faces]
        inner = residual[1:-1]
        applied = inner + diagonal[1:-1] * inner - stencil(residual, narrow, 0)
        alpha, beta = weight_rows()
        j = block * fine + k
        return values[2:-2] + alpha[j : j + 1] * inner - beta[j : j + 1] * applied

    def landing(kind):
        target = (advanced_ref, final_ref)[kind]
        if rows % 8 == 0:
            return target.at[0, :, pl.ds(pl.multiple_of(mine * rows, 8), rows)]
        return back.at[kind, mine]

    def landed(kind):
        target = (advanced_ref, final_ref)[kind]
        drain(target if rows % 8 == 0 else back.at[kind], out_sem.at[2 * blocks + kind])
        if rows % 8:
            unpack(target, kind)

    def deliver(slot, owner_block, value):
        outs[slot] = jnp.swapaxes(value, 0, 1).reshape(slabs, layers, rows, nz)
        kind = slot // blocks

        def send(step, _):
            target = (space + step) % slabs
            pltpu.make_async_remote_copy(
                outs.at[slot, target], landing(kind), out_sem.at[slot], out_sem.at[2 * blocks + kind],
                device_id={"space": target, "tm": owner_block}, device_id_type=MESH,
            ).start()
            return 0

        lax.fori_loop(1, slabs, send, 0)

        @pl.when(time == owner_block)
        def _():
            pltpu.make_async_copy(
                outs.at[slot, space], landing(kind), out_sem.at[2 * blocks + kind]
            ).start()

        @pl.when(time != owner_block)
        def _():
            pltpu.make_async_remote_copy(
                outs.at[slot, space], landing(kind), out_sem.at[slot], out_sem.at[2 * blocks + kind],
                device_id={"tm": owner_block}, device_id_type=MESH,
            ).start()

    def settled(slot, owner_block):
        drain(outs.at[slot, 0 : slabs - 1], out_sem.at[slot])

        @pl.when(time != owner_block)
        def _():
            drain(outs.at[slot, 0], out_sem.at[slot])

    def trim(values, off):
        low = width - off
        return values[low : low + rows]

    exchange = 0
    current = [raw[4 + block] for block in range(blocks)]
    off = 0
    live = list(range(blocks))
    exchanges = []
    for step in range(2 * fine - 1):
        second = step >= fine
        k = step - fine if second else step
        if step == fine:
            live = [blocks - 1]
        if step and (off + 2 > width):
            for block in live:
                states[exchange, block, inside] = trim(current[block], off)
            part = states.at[exchange, live[0] : live[-1] + 1]
            cuts = (
                part.at[:, rows : rows + width], part.at[:, 0:width],
                part.at[:, width : 2 * width], part.at[:, width + rows : ext],
            )
            swap(exchange + 2, *cuts)
            arrived(exchange + 2, cuts[1], cuts[3])
            exchanges.append((exchange + 2, cuts))
            for block in live:
                current[block] = states[exchange, block]
            off = 0
            exchange += 1
        for block in live:
            current[block] = advance(current[block], off, block, k)
        off += 2
        if step == fine - 2:
            deliver(blocks, 0, trim(current[0], off))
        if step == fine - 1:
            for block in range(blocks):
                deliver(block, block, trim(current[block], off))
            current[1] = current[0]
    deliver(blocks + 1, 1, trim(current[1], off))

    def unpack(dest, kind):
        for layer in range(layers):
            for core in range(cores):
                dest[0, layer, core * rows : (core + 1) * rows] = back[kind, core, layer]

    landed(0)
    sent(0, coef_views[0], coef_views[2])
    sent(1, state_views[0], state_views[2])
    for index, cuts in exchanges:
        sent(index, cuts[0], cuts[2])
    drain(recvc.at[0 : slabs - 1], a2a_sem.at[0])
    drain(recvs.at[0 : cores - 1], a2a_sem.at[2])
    drain(gath.at[0 : cores - 1], gath_sem.at[0])
    for kind in range(2):
        for block in range(blocks):
            settled(kind * blocks + block, block)
    landed(1)


def solution(mesh):
    slabs = mesh.shape["space"]
    blocks = mesh.shape["tm"]

    def shards(initial, source, diffusion, wind_field, buildings, strength):
        layers, ny, nz = diffusion.shape
        nx = layers * slabs
        cores = slabs * blocks
        rows = ny // cores
        fine = strength.shape[1]
        width = 8 if rows >= 8 else 2
        per = width // 2
        groups = -(-(2 * fine - 1) // per) - 1
        ext = rows + 2 * width
        f32 = jnp.float32
        return pl.pallas_call(
            functools.partial(kernel, slabs, blocks, rows, width, per, groups),
            out_shape=[jax.ShapeDtypeStruct(initial.shape, f32)] * 2,
            in_specs=[pl.BlockSpec(memory_space=pltpu.HBM)] * 6,
            out_specs=[pl.BlockSpec(memory_space=pltpu.HBM if rows % 8 == 0 else pltpu.VMEM)] * 2,
            scratch_shapes=[
                pltpu.VMEM(initial.shape, f32),
                pltpu.VMEM(source.shape, source.dtype),
                pltpu.VMEM(diffusion.shape, f32),
                pltpu.VMEM(wind_field.shape, f32),
                pltpu.VMEM(buildings.shape, buildings.dtype),
                pltpu.VMEM(strength.shape, f32),
                pltpu.VMEM((cores, 4, layers, rows, nz), f32),
                pltpu.VMEM((cores, 2, layers, rows, nz), f32),
                pltpu.VMEM((slabs, 4, layers, rows, nz), f32),
                pltpu.VMEM((cores, 2, layers, rows, nz), f32),
                pltpu.VMEM((4 + 2 * blocks, ext, nx, nz), f32),
                pltpu.VMEM((groups, blocks, ext, nx, nz), f32),
                pltpu.VMEM((blocks, fine, 8, nz), f32),
                pltpu.VMEM((cores, blocks * fine, nz), f32),
                pltpu.VMEM((2 * blocks, slabs, layers, rows, nz), f32),
                pltpu.VMEM((2, cores if rows % 8 else 1, layers, rows, nz), f32),
                pltpu.SemaphoreType.DMA((6,)),
                pltpu.SemaphoreType.DMA((4,)),
                pltpu.SemaphoreType.DMA((2,)),
                pltpu.SemaphoreType.DMA((2,)),
                pltpu.SemaphoreType.DMA((groups + 2, 2)),
                pltpu.SemaphoreType.DMA((groups + 2, 2)),
                pltpu.SemaphoreType.DMA((2 * blocks + 2,)),
            ],
            compiler_params=pltpu.CompilerParams(
                collective_id=0, has_side_effects=True, vmem_limit_bytes=63 << 20
            ),
        )(initial, source, diffusion, wind_field, buildings, strength)

    in_specs = (
        P(("copy", "tm"), "space", None, None),
        P(("copy", "tm"), "space", None, None),
        P("space", None, None),
        P(None, "space", None, None),
        P("space", None, None),
        P("tm", None),
    )
    out_specs = (P(("copy", "tm"), "space", None, None), P(("copy", "tm"), "space", None, None))
    return jax.shard_map(shards, mesh=mesh, in_specs=in_specs, out_specs=out_specs, check_vma=False)
```
